256 devices in a mesh: gx: 8 (over z), gy: 32 (over y, x, core).
Axes of the slice: x: 4, y: 4, z: 8, core: 2. Of those that a mesh axis runs over, the one named last changes fastest.
Arguments:
- movie: bfloat16 [64, 256, 128, 128], P('gx', 'gy'), may hold values from -14 to 14
- brain_mask: int32 [64, 256, 128], P('gx', 'gy'), may hold values 0 or 1
Outputs:
- fitted: bfloat16 [64, 256, 128, 128], P('gx', 'gy')
- propagator: float32 [127, 127], replicated
The draws below stay inside these ranges and needn't reach their ends.
All inputs are finite; a program needn't handle non-finite values. No bound on the sum of `brain_mask` on one device may be relied on, other than what follows from the above.
Results may differ from the reference program's by a relative error of at most 0.00095.
Values may be sent and summed in bfloat16 or wider, within the bound.
No kernel may reach another device: no remote copies, remote signals or barrier semaphores. Data moves between devices by JAX's collectives and lax.ppermute only.
A program may use at most 128 MiB of HBM per device.

```python
import math
import jax
import jax.numpy as jnp
from jax import lax

FR = 128
RAD = 4
CX = 8
CY = 8
CZ = 128
NX = 64
NY = 256
NZ = 128


def draw_movie(key, part):
    key_shift = jax.random.fold_in(key, 11)
    key_amp = jax.random.fold_in(key, 12)
    key_sign = jax.random.fold_in(key, 13)
    key_phase = jax.random.fold_in(key, 14)
    key_noise = jax.random.fold_in(key, 15)
    key_smooth = jax.random.fold_in(key, 16)
    key_heading = jax.random.fold_in(key, 17)
    key_offset = jax.random.fold_in(key, 18)
    half_frames = FR // 2
    columns = NY // CY
    shift = jax.random.randint(key_shift, (), 0, half_frames)
    brick_x = jnp.arange(NX) // CX
    brick_y = jnp.arange(NY) // CY
    brick = brick_x[:, None] * columns + brick_y[None, :]
    freq_index = ((brick + shift) % half_frames).astype(jnp.float32)
    omega = math.pi * (freq_index + 0.5) / half_frames
    rise = brick_y.astype(jnp.float32) / max(columns - 1, 1)
    scale_col = jnp.exp(math.log(3.0) * rise)
    amp = jax.random.uniform(key_amp, (NX, NY, NZ), jnp.float32, 0.5, 1.5)
    noise = 0.4 * jnp.clip(jax.random.normal(key_noise, (NX, NY, NZ, FR), jnp.float32), -3.0, 3.0)
    sign = 2.0 * jax.random.bernoulli(key_sign, 0.5, (NX, NY, NZ)).astype(jnp.float32) - 1.0
    phase = jax.random.uniform(key_phase, (NX, NY, NZ), jnp.float32, -math.pi, math.pi)
    times = jnp.arange(FR).astype(jnp.float32)
    wave = jnp.cos(omega[:, :, None, None] * times[None, None, None, :] + phase[:, :, :, None])
    slow_index = jax.random.randint(key_smooth, (), 0, half_frames).astype(jnp.float32)
    slow_omega = math.pi * (slow_index + 0.25) / half_frames
    heading = 2.0 * jax.random.bernoulli(key_heading, 0.5, (3,)).astype(jnp.float32) - 1.0
    offset = jax.random.uniform(key_offset, (), jnp.float32, -math.pi, math.pi)
    across = 2.0 * math.pi / (8.0 * RAD)
    along = 2.0 * math.pi / (16.0 * RAD)
    pos_x = jnp.arange(NX).astype(jnp.float32)
    pos_y = jnp.arange(NY).astype(jnp.float32)
    pos_z = jnp.arange(NZ).astype(jnp.float32)
    spatial = heading[0] * across * pos_x[:, None, None] + heading[1] * across * pos_y[None, :, None] + heading[2] * along * pos_z[None, None, :] + offset
    smooth_part = 1.2 * jnp.cos(spatial[:, :, :, None] + slow_omega * times[None, None, None, :])
    value = scale_col[None, :, None, None] * (1.5 * (amp * sign)[:, :, :, None] * wave + noise + smooth_part)
    return value.astype(jnp.bfloat16)


def set_ends(entries, stream_key, smallest, largest):
    spot = [jax.random.randint(jax.random.fold_in(stream_key, axis), (), 0, length) for axis, length in enumerate(entries.shape)]
    widest = entries.shape.index(max(entries.shape))
    neighbour = spot[:widest] + [(spot[widest] + 1) % entries.shape[widest]] + spot[widest + 1:]
    return entries.at[tuple(spot)].set(smallest).at[tuple(neighbour)].set(largest)


def setup_inputs(seed: int = 0) -> dict:
    streams_of = jax.random.split(jax.random.key(seed), 3)
    return {
        "movie": draw_movie(jax.random.fold_in(streams_of[2], 71), 0),
        "brain_mask": set_ends((jax.random.randint(streams_of[1], (NX, NY, NZ), 0, 4) < 3).astype(jnp.int32), jax.random.fold_in(streams_of[1], 1), 0, 1),
    }


def kernel_weights():
    offsets = jnp.arange(-RAD, RAD + 1).astype(jnp.float32)
    sigma = RAD / 2.0
    raw = jnp.exp(-offsets * offsets / (2.0 * sigma * sigma))
    return raw / jnp.sum(raw)

def blur_axis(field, axis, weights, length):
    widths = [(0, 0)] * field.ndim
    widths[axis] = (RAD, RAD)
    padded = jnp.pad(field, widths)
    total = jnp.zeros(field.shape, jnp.float32)
    for k in range(2 * RAD + 1):
        total = total + weights[k] * lax.slice_in_dim(padded, k, k + length, axis=axis)
    return total

def chol_solve(factor, right):
    middle = lax.linalg.triangular_solve(factor, right, left_side=True, lower=True)
    return lax.linalg.triangular_solve(factor, middle, left_side=True, lower=True, transpose_a=True)

def reference(movie, brain_mask):
    weights = kernel_weights()
    nblk = FR // 8
    blocks = jnp.moveaxis(movie.reshape(NX, NY, NZ, nblk, 8), 3, 0)
    mask_f = brain_mask.astype(jnp.float32)[:, :, :, None]

    def filter_block(block):
        field = block.astype(jnp.float32)
        blur = blur_axis(field, 2, weights, NZ)
        blur = blur_axis(blur, 1, weights, NY)
        blur = blur_axis(blur, 0, weights, NX)
        return mask_f * (field - blur)
    filtered = lax.map(filter_block, blocks)
    filtered = jnp.moveaxis(filtered, 0, 3).reshape(NX * NY * NZ, FR)
    rows_blk = CX * CY * CZ
    row_blocks = filtered.reshape(-1, rows_blk, FR)

    def add_gram(total, rows):
        part = lax.dot_general(rows.astype(jnp.float32), rows.astype(jnp.float32), (((0,), (0,)), ((), ())), precision=lax.Precision.HIGHEST, preferred_element_type=jnp.float32)
        return (total + part, None)
    gram, _ = lax.scan(add_gram, jnp.zeros((FR, FR), jnp.float32), row_blocks)
    g_left = gram[:FR - 1, :FR - 1]
    g_right = gram[:FR - 1, 1:]
    lam = 0.5 * jnp.trace(g_left) / (FR - 1)
    factor = jnp.linalg.cholesky(g_left + lam * jnp.eye(FR - 1, dtype=jnp.float32))
    propagator = chol_solve(factor, g_right)
    advance = jnp.zeros((FR, FR), jnp.float32)
    advance = advance.at[0, 0].set(1.0)
    advance = advance.at[:FR - 1, 1:].set(propagator)

    def fit_block(rows):
        return jnp.dot(rows.astype(jnp.float32), advance.astype(jnp.float32), precision=lax.Precision.HIGHEST, preferred_element_type=jnp.float32).astype(jnp.bfloat16)
    fitted = lax.map(fit_block, row_blocks).reshape(NX, NY, NZ, FR)
    return (fitted, propagator)
```

```python
import jax
import jax.numpy as jnp
from jax import lax
from jax.sharding import Mesh, PartitionSpec as P

RAD = 4


def extended(x, sides, width):
    for axis, dim in sides:
        peers, length = (lax.axis_size(axis), x.shape[dim])
        up = [(i, (i + 1) % peers) for i in range(peers - 1)]
        down = [(j, i) for i, j in up]
        last = lax.slice_in_dim(x, length - width, length, axis=dim)
        initial = lax.slice_in_dim(x, 0, width, axis=dim)
        before = lax.ppermute(last, axis, up)
        after = lax.ppermute(initial, axis, down)
        x = jnp.concatenate([before, x, after], axis=dim)
    return x


def kernel_weights():
    offsets = jnp.arange(-RAD, RAD + 1).astype(jnp.float32)
    sigma = RAD / 2.0
    raw = jnp.exp(-offsets * offsets / (2.0 * sigma * sigma))
    return raw / jnp.sum(raw)


def taps_along(field, axis, weights, length):
    total = jnp.zeros(field.shape[:axis] + (length,) + field.shape[axis + 1 :], jnp.float32)
    for k in range(2 * RAD + 1):
        total = total + weights[k] * lax.slice_in_dim(field, k, k + length, axis=axis)
    return total


def chol_solve(factor, right):
    middle = lax.linalg.triangular_solve(factor, right, left_side=True, lower=True)
    return lax.linalg.triangular_solve(factor, middle, left_side=True, lower=True, transpose_a=True)


def shifted(value, axis, step):
    size = lax.axis_size(axis)
    return lax.ppermute(value, axis, [((i + step) % size, i) for i in range(size)])


def ring_sum(value, axis):
    size = lax.axis_size(axis)
    if size == 8:
        right, left = shifted(value, axis, 1), shifted(value, axis, -1)
        pair = value + right
        three = pair + left
        ahead, behind = shifted(three, axis, 3), shifted(pair, axis, -3)
        return three + (ahead + behind)
    parts = [shifted(value, axis, step) for step in range(1, size)]
    for part in parts:
        value = value + part
    return value


def grid_sum(value):
    for axis in ("c", "x", "y", "z"):
        value = ring_sum(value, axis)
    return value


def on_device(movie, brain_mask):
    size_x, size_y, size_z, frames = movie.shape
    weights = kernel_weights()
    padded = extended(movie, (("z", 0), (("y", "x", "c"), 1)), RAD)
    wide = jnp.pad(padded.astype(jnp.float32), ((0, 0), (0, 0), (RAD, RAD), (0, 0)))
    blur = taps_along(wide, 2, weights, size_z)
    blur = taps_along(blur, 1, weights, size_y)
    blur = taps_along(blur, 0, weights, size_x)
    mask_f = brain_mask.astype(jnp.float32)[:, :, :, None]
    filtered = (mask_f * (movie.astype(jnp.float32) - blur)).reshape(-1, frames)
    local_gram = lax.dot_general(
        filtered,
        filtered,
        (((0,), (0,)), ((), ())),
        precision=lax.Precision.HIGHEST,
        preferred_element_type=jnp.float32,
    )
    gram = grid_sum(local_gram)
    g_left = gram[: frames - 1, : frames - 1]
    g_right = gram[: frames - 1, 1:]
    lam = 0.5 * jnp.trace(g_left) / (frames - 1)
    factor = jnp.linalg.cholesky(g_left + lam * jnp.eye(frames - 1, dtype=jnp.float32))
    propagator = chol_solve(factor, g_right)
    advance = jnp.zeros((frames, frames), jnp.float32)
    advance = advance.at[0, 0].set(1.0)
    advance = advance.at[: frames - 1, 1:].set(propagator)
    fitted = jnp.dot(
        filtered, advance, precision=lax.Precision.HIGHEST, preferred_element_type=jnp.float32
    )
    fitted = fitted.astype(jnp.bfloat16).reshape(size_x, size_y, size_z, frames)
    return (fitted, propagator)


def solution(mesh):
    grid = Mesh(mesh.devices.reshape(8, 4, 4, 2), ("z", "y", "x", "c"))
    across = ("y", "x", "c")
    return jax.shard_map(
        on_device,
        mesh=grid,
        in_specs=(P("z", across, None, None), P("z", across, None)),
        out_specs=(P("z", across, None, None), P()),
        check_vma=False,
    )
```

```python
import functools

import jax
import jax.numpy as jnp
import numpy as np
from jax import lax
from jax.experimental import pallas as pl
from jax.experimental.pallas import tpu as pltpu
from jax.sharding import Mesh, PartitionSpec as P

RAD = 4
F32, BF16 = jnp.float32, jnp.bfloat16


def tap_weights():
    offsets = np.arange(-RAD, RAD + 1).astype(np.float64)
    sigma = RAD / 2.0
    raw = np.exp(-offsets * offsets / (2.0 * sigma * sigma))
    return (raw / raw.sum()).astype(np.float32)


WEIGHTS = tap_weights()
TAPS = [float(w) for w in WEIGHTS[RAD:]]


def band_matrix(size):
    band = np.zeros((size, size), np.float32)
    for k in range(-RAD, RAD + 1):
        band += np.diag(np.full(size - abs(k), WEIGHTS[k + RAD]), k)
    return band


def from_before(value, axis):
    size = lax.axis_size(axis)
    return lax.ppermute(value, axis, [(i, i + 1) for i in range(size - 1)])


def from_after(value, axis):
    size = lax.axis_size(axis)
    return lax.ppermute(value, axis, [(i + 1, i) for i in range(size - 1)])


def shifted(value, axis, step):
    size = lax.axis_size(axis)
    return lax.ppermute(value, axis, [((i + step) % size, i) for i in range(size)])


def ring_sum(value, axis):
    size = lax.axis_size(axis)
    if size == 8:
        right, left = shifted(value, axis, 1), shifted(value, axis, -1)
        pair = value + right
        three = pair + left
        ahead, behind = shifted(three, axis, 3), shifted(pair, axis, -3)
        return three + (ahead + behind)
    parts = [shifted(value, axis, step) for step in range(1, size)]
    for part in parts:
        value = value + part
    return value


def grid_sum(value):
    for axis in ("c", "x", "y", "z"):
        value = ring_sum(value, axis)
    return value


def taps_line(line, first, count):
    out = []
    for i in range(first, first + count):
        total = None
        for k, weight in enumerate(TAPS):
            pair = [line[j] for j in sorted({i - k, i + k}) if j in line]
            if not pair:
                continue
            term = (pair[0] if len(pair) == 1 else pair[0] + pair[1]) * weight
            total = term if total is None else total + term
        out.append(total)
    return out


def faces_kernel(own, y_before, y_after, x_before, x_after, out, rows, *, depth):
    size_x, size_y = own.shape[:2]

    @pl.loop(0, depth // 8)
    def _(step):
        z = pl.ds(pl.multiple_of(step * 8, 8), 8)

        def load(ref, i, j):
            return ref[i, j, z, :].astype(F32)

        for i in range(-RAD, size_x + RAD):
            if 0 <= i < size_x:
                line = {j: load(own, i, j) for j in range(size_y)}
                line |= {j - RAD: load(y_before, i, j) for j in range(RAD)}
                line |= {j + size_y: load(y_after, i, j) for j in range(RAD)}
            elif i < 0:
                line = {j: load(x_before, i + RAD, j) for j in range(size_y)}
            else:
                line = {j: load(x_after, i - size_x, j) for j in range(size_y)}
            for j, value in enumerate(taps_line(line, 0, size_y)):
                rows[i + RAD, j] = value
        for j in range(size_y):
            line = {i: rows[i + RAD, j] for i in range(-RAD, size_x + RAD)}
            for i, value in enumerate(taps_line(line, 0, size_x)):
                out[i, j, z, :] = value


def faces(own, y_before, y_after, x_before, x_after):
    size_x, size_y, size_z, frames = own.shape
    depth = 32
    spec = lambda a, b: pl.BlockSpec((a, b, depth, frames), lambda i: (0, 0, i, 0))
    return pl.pallas_call(
        functools.partial(faces_kernel, depth=depth),
        grid=(size_z // depth,),
        in_specs=[
            spec(size_x, size_y),
            spec(size_x, RAD),
            spec(size_x, RAD),
            spec(RAD, size_y),
            spec(RAD, size_y),
        ],
        out_specs=spec(size_x, size_y),
        out_shape=jax.ShapeDtypeStruct(own.shape, F32),
        scratch_shapes=[pltpu.VMEM((size_x + 2 * RAD, size_y, 8, frames), F32)],
        compiler_params=pltpu.CompilerParams(vmem_limit_bytes=32 << 20),
        cost_estimate=pl.CostEstimate(
            flops=60_000_000, bytes_accessed=10 << 20, transcendentals=0
        ),
        name="faces",
    )(own, y_before, y_after, x_before, x_after)


def split(value):
    high = value.astype(BF16)
    return high, (value - high.astype(F32)).astype(BF16)


def filter_kernel(
    table, part, own, mask, c_before, c_after, left, low, high_out, low_out, gram, total
):
    step = pl.program_id(0)
    size_y, size_z, frames = own.shape[1:]

    @pl.when(step == 0)
    def _():
        total[...] = jnp.zeros_like(total)

    weights = [table[step, r] for r in range(RAD)]

    def combined(ref, j):
        value = ref[0, j].astype(F32) * weights[0]
        for r in range(1, RAD):
            value = value + ref[r, j].astype(F32) * weights[r]
        return value

    before = {j - RAD: combined(c_before, j) for j in range(RAD)}
    after = {j + size_y: combined(c_after, j) for j in range(RAD)}

    def column(j):
        value = part[0, j]
        for i, line in (before | after).items():
            if abs(i - j) <= RAD:
                value = value + line * TAPS[abs(i - j)]
        return value

    for j in range(0, size_y, 2):
        pair = jnp.concatenate([column(j), column(j + 1)], axis=1)
        high, rest = split(pair)
        blur = jnp.dot(
            left[...], jnp.concatenate([high, rest], axis=0), preferred_element_type=F32
        ) + jnp.dot(low[...], high, preferred_element_type=F32)
        for q in range(2):
            value = own[0, j + q].astype(F32) - blur[:, q * frames : (q + 1) * frames]
            value = value * mask[0, :, j + q : j + q + 1]
            high, rest = split(value)
            high_out[0, j + q] = high
            low_out[0, j + q] = rest
    high = high_out[0].reshape(size_y * size_z, frames)
    rest = low_out[0].reshape(size_y * size_z, frames)
    total[...] += lax.dot_general(
        high,
        jnp.concatenate([high, rest], axis=1),
        (((0,), (0,)), ((), ())),
        preferred_element_type=F32,
    )

    @pl.when(step == pl.num_programs(0) - 1)
    def _():
        cross = total[:, frames:]
        gram[...] = total[:, :frames] + (cross + cross.T)


def filter_and_gram(part, own, mask, c_before, c_after):
    size_x, size_y, size_z, frames = own.shape
    band = band_matrix(size_z)
    high = band.astype(jnp.bfloat16)
    low = (band - high.astype(np.float32)).astype(jnp.bfloat16)
    left = np.concatenate([high, high], axis=1)
    table = np.zeros((size_x, RAD), np.float32)
    for i in range(size_x):
        for r in range(RAD):
            place = r - RAD if i < RAD else size_x + r
            if abs(place - i) <= RAD:
                table[i, r] = WEIGHTS[RAD + abs(place - i)]
    slab = pl.BlockSpec((1, size_y, size_z, frames), lambda i: (i, 0, 0, 0))
    side = pl.BlockSpec((RAD, RAD, size_z, frames), lambda i: (i // RAD, 0, 0, 0))
    whole = lambda a, b: pl.BlockSpec((a, b), lambda i: (0, 0))
    half = jax.ShapeDtypeStruct(own.shape, BF16)
    return pl.pallas_call(
        filter_kernel,
        grid=(size_x,),
        in_specs=[
            pl.BlockSpec(memory_space=pltpu.SMEM),
            slab,
            slab,
            pl.BlockSpec((1, size_z, size_y), lambda i: (i, 0, 0)),
            side,
            side,
            whole(size_z, 2 * size_z),
            whole(size_z, size_z),
        ],
        out_specs=[slab, slab, whole(frames, frames)],
        out_shape=[half, half, jax.ShapeDtypeStruct((frames, frames), F32)],
        scratch_shapes=[pltpu.VMEM((frames, 2 * frames), F32)],
        compiler_params=pltpu.CompilerParams(vmem_limit_bytes=32 << 20),
        cost_estimate=pl.CostEstimate(
            flops=3_000_000_000, bytes_accessed=13 << 20, transcendentals=0
        ),
        name="filter",
    )(
        jnp.asarray(table),
        part,
        own,
        mask,
        c_before,
        c_after,
        jnp.asarray(left),
        jnp.asarray(low),
    )


def solve_kernel(gram, advance):
    size = gram.shape[0]
    g = gram[...]
    row = lax.broadcasted_iota(jnp.int32, (size, size), 0)
    lane = lax.broadcasted_iota(jnp.int32, (size, size), 1)
    last = size - 1
    inside = (row < last) & (lane < last)
    diagonal = row == lane
    trace = jnp.sum(jnp.where(diagonal & inside, g, 0.0), axis=(0, 1), keepdims=True)
    lam = trace * (0.5 / last)
    a = jnp.where(inside, g, 0.0) + jnp.where(
        diagonal, jnp.where(row < last, lam, 1.0), 0.0
    )
    wide = jnp.concatenate([a, g], axis=1)
    tiles = [wide[8 * t : 8 * t + 8] for t in range(size // 8)]
    inner = lax.broadcasted_iota(jnp.int32, (8, 2 * size), 0)
    for k in range(last):
        t, s = divmod(k, 8)
        line = tiles[t][s : s + 1] * (1.0 / tiles[t][s : s + 1, k : k + 1])
        tiles = [tile - tile[:, k : k + 1] * line for tile in tiles[:t]] + [
            jnp.where(inner == s, line, tiles[t] - tiles[t][:, k : k + 1] * line)
        ] + [tile - tile[:, k : k + 1] * line for tile in tiles[t + 1 :]]
    b = jnp.concatenate(tiles, axis=0)[:, size:]
    solved = jnp.where(row < last, b, 0.0)
    advance[...] = jnp.where(lane == 0, jnp.where(row == 0, 1.0, 0.0), solved)


def solve(gram):
    return pl.pallas_call(
        solve_kernel,
        out_shape=jax.ShapeDtypeStruct(gram.shape, F32),
        name="solve",
    )(gram)


def fit_kernel(high, low, advance, out):
    m_high, m_low = split(advance[...])
    both = jnp.dot(
        high[...],
        jnp.concatenate([m_high, m_low], axis=1),
        preferred_element_type=F32,
    )
    frames = m_high.shape[0]
    rest = jnp.dot(low[...], m_high, preferred_element_type=F32)
    out[...] = (both[:, :frames] + (both[:, frames:] + rest)).astype(BF16)


def fit(high, low, advance):
    rows, frames = high.shape
    block = 1024
    spec = pl.BlockSpec((block, frames), lambda i: (i, 0))
    return pl.pallas_call(
        fit_kernel,
        grid=(rows // block,),
        in_specs=[spec, spec, pl.BlockSpec((frames, frames), lambda i: (0, 0))],
        out_specs=spec,
        out_shape=jax.ShapeDtypeStruct((rows, frames), BF16),
        name="fit",
    )(high, low, advance)


def on_device(movie, brain_mask):
    size_x, size_y, size_z, frames = movie.shape
    across = ("y", "x", "c")
    x_before = from_before(movie[size_x - RAD :], "z")
    x_after = from_after(movie[:RAD], "z")
    y_before = from_before(movie[:, size_y - RAD :], across)
    y_after = from_after(movie[:, :RAD], across)
    mask = jnp.swapaxes(brain_mask, 1, 2).astype(F32)
    c_before = from_before(
        jnp.concatenate([x_before[:, size_y - RAD :], x_after[:, size_y - RAD :]], 0),
        across,
    )
    c_after = from_after(
        jnp.concatenate([x_before[:, :RAD], x_after[:, :RAD]], 0), across
    )
    part = faces(movie, y_before, y_after, x_before, x_after)
    high, low, gram = filter_and_gram(part, movie, mask, c_before, c_after)
    gram = grid_sum(gram)
    advance = solve(gram)
    rows = size_x * size_y * size_z
    fitted = fit(high.reshape(rows, frames), low.reshape(rows, frames), advance)
    return fitted.reshape(movie.shape), advance[: frames - 1, 1:]


def solution(mesh):
    grid = Mesh(mesh.devices.reshape(8, 4, 4, 2), ("z", "y", "x", "c"))
    across = ("y", "x", "c")
    return jax.shard_map(
        on_device,
        mesh=grid,
        in_specs=(P("z", across, None, None), P("z", across, None)),
        out_specs=(P("z", across, None, None), P()),
        check_vma=False,
    )
```

```python
import functools

import jax
import jax.numpy as jnp
import numpy as np
from jax import lax
from jax.experimental import pallas as pl
from jax.experimental.pallas import tpu as pltpu
from jax.sharding import Mesh, PartitionSpec as P

RAD = 4
F32, BF16 = jnp.float32, jnp.bfloat16


def tap_weights():
    offsets = np.arange(-RAD, RAD + 1).astype(np.float64)
    sigma = RAD / 2.0
    raw = np.exp(-offsets * offsets / (2.0 * sigma * sigma))
    return (raw / raw.sum()).astype(np.float32)


WEIGHTS = tap_weights()
TAPS = [float(w) for w in WEIGHTS[RAD:]]


def band_matrix(size):
    band = np.zeros((size, size), np.float32)
    for k in range(-RAD, RAD + 1):
        band += np.diag(np.full(size - abs(k), WEIGHTS[k + RAD]), k)
    return band


def from_before(value, axis):
    size = lax.axis_size(axis)
    return lax.ppermute(value, axis, [(i, i + 1) for i in range(size - 1)])


def from_after(value, axis):
    size = lax.axis_size(axis)
    return lax.ppermute(value, axis, [(i + 1, i) for i in range(size - 1)])


ROUNDS = (
    ("c", 1),
    ("x", 1),
    ("x", 3),
    ("y", 1),
    ("y", 3),
    ("z", 1),
    ("z", 2),
    ("z", 6),
)


def grid_sum(value):
    for axis, flip in ROUNDS:
        size = lax.axis_size(axis)
        value = value + lax.ppermute(value, axis, [(i, i ^ flip) for i in range(size)])
    return value


def taps_line(line, first, count):
    out = []
    for i in range(first, first + count):
        total = None
        for k, weight in enumerate(TAPS):
            pair = [line[j] for j in sorted({i - k, i + k}) if j in line]
            if not pair:
                continue
            term = (pair[0] if len(pair) == 1 else pair[0] + pair[1]) * weight
            total = term if total is None else total + term
        out.append(total)
    return out


def faces_kernel(
    own, y_before, y_after, before_low, before_high, after_low, after_high, out, rows, *, depth
):
    size_x, size_y = own.shape[:2]

    @pl.loop(0, depth // 8)
    def _(step):
        z = pl.ds(pl.multiple_of(step * 8, 8), 8)

        def load(ref, i, j):
            return ref[i, j, z, :].astype(F32)

        def load_line(low, high, i):
            return {
                j: load(low, i, j) if j < RAD else load(high, i, j - RAD)
                for j in range(size_y)
            }

        for i in range(-RAD, size_x + RAD):
            if 0 <= i < size_x:
                line = {j: load(own, i, j) for j in range(size_y)}
                line |= {j - RAD: load(y_before, i, j) for j in range(RAD)}
                line |= {j + size_y: load(y_after, i, j) for j in range(RAD)}
            elif i < 0:
                line = load_line(before_low, before_high, i + RAD)
            else:
                line = load_line(after_low, after_high, i - size_x)
            for j, value in enumerate(taps_line(line, 0, size_y)):
                rows[i + RAD, j] = value
        for j in range(size_y):
            line = {i: rows[i + RAD, j] for i in range(-RAD, size_x + RAD)}
            for i, value in enumerate(taps_line(line, 0, size_x)):
                out[i, j, z, :] = value


def faces(own, y_before, y_after, before_low, before_high, after_low, after_high):
    size_x, size_y, size_z, frames = own.shape
    depth = 32
    spec = lambda a, b: pl.BlockSpec((a, b, depth, frames), lambda i: (0, 0, i, 0))
    return pl.pallas_call(
        functools.partial(faces_kernel, depth=depth),
        grid=(size_z // depth,),
        in_specs=[spec(size_x, size_y)]
        + [spec(size_x, RAD)] * 2
        + [spec(RAD, size_y - RAD)] * 4,
        out_specs=spec(size_x, size_y),
        out_shape=jax.ShapeDtypeStruct(own.shape, F32),
        scratch_shapes=[pltpu.VMEM((size_x + 2 * RAD, size_y, 8, frames), F32)],
        compiler_params=pltpu.CompilerParams(vmem_limit_bytes=16 << 20),
        cost_estimate=pl.CostEstimate(
            flops=60_000_000, bytes_accessed=10 << 20, transcendentals=0
        ),
        name="faces",
    )(own, y_before, y_after, before_low, before_high, after_low, after_high)


def split(value):
    high = value.astype(BF16)
    return high, (value - high.astype(F32)).astype(BF16)


def pack(full):
    size = full.shape[0]
    half = size // 2
    row = lax.broadcasted_iota(jnp.int32, (half, size), 0)
    lane = lax.broadcasted_iota(jnp.int32, (half, size), 1)
    moved = pltpu.roll(full[half:], half, 1)
    diagonal = jnp.sum(jnp.where(row == lane, moved, 0.0), axis=0, keepdims=True)
    return jnp.concatenate(
        [
            jnp.where(lane >= row, full[:half], moved),
            jnp.broadcast_to(diagonal, (8, size)),
        ],
        axis=0,
    )


def unpack(packed, row, lane):
    size = packed.shape[1]
    half = size // 2
    top = packed[:half]
    moved = pltpu.roll(top, half, 1)
    inner_row = lax.broadcasted_iota(jnp.int32, (half, size), 0)
    inner_lane = lax.broadcasted_iota(jnp.int32, (half, size), 1)
    diagonal = pltpu.roll(jnp.broadcast_to(packed[half : half + 1], (half, size)), half, 1)
    bottom = jnp.where(inner_lane == inner_row + half, diagonal, moved)
    known = jnp.concatenate([top, bottom], axis=0)
    held = ((row < half) & (lane >= row)) | (
        (row >= half) & (lane >= half) & (lane <= row)
    )
    return jnp.where(held, known, known.T)


def filter_kernel(
    table, part, own, mask, c_before, c_after, left, low, high_out, low_out, gram, total
):
    step = pl.program_id(0)
    size_y, size_z, frames = own.shape[1:]

    @pl.when(step == 0)
    def _():
        total[...] = jnp.zeros_like(total)

    weights = [table[step, r] for r in range(RAD)]

    def combined(ref, j):
        value = ref[0, j].astype(F32) * weights[0]
        for r in range(1, RAD):
            value = value + ref[r, j].astype(F32) * weights[r]
        return value

    before = {j - RAD: combined(c_before, j) for j in range(RAD)}
    after = {j + size_y: combined(c_after, j) for j in range(RAD)}

    def column(j):
        value = part[0, j]
        for i, line in (before | after).items():
            if abs(i - j) <= RAD:
                value = value + line * TAPS[abs(i - j)]
        return value

    for j in range(0, size_y, 2):
        pair = jnp.concatenate([column(j), column(j + 1)], axis=1)
        high, rest = split(pair)
        blur = jnp.dot(
            left[...], jnp.concatenate([high, rest], axis=0), preferred_element_type=F32
        ) + jnp.dot(low[...], high, preferred_element_type=F32)
        for q in range(2):
            value = own[0, j + q].astype(F32) - blur[:, q * frames : (q + 1) * frames]
            value = value * mask[0, :, j + q : j + q + 1]
            high, rest = split(value)
            high_out[0, j + q] = high
            low_out[0, j + q] = rest
    high = high_out[0].reshape(size_y * size_z, frames)
    rest = low_out[0].reshape(size_y * size_z, frames)
    total[...] += lax.dot_general(
        high,
        jnp.concatenate([high, rest], axis=1),
        (((0,), (0,)), ((), ())),
        preferred_element_type=F32,
    )

    @pl.when(step == pl.num_programs(0) - 1)
    def _():
        cross = total[:, frames:]
        gram[...] = pack(total[:, :frames] + (cross + cross.T))


def filter_and_gram(part, own, mask, c_before, c_after):
    size_x, size_y, size_z, frames = own.shape
    band = band_matrix(size_z)
    high = band.astype(jnp.bfloat16)
    low = (band - high.astype(np.float32)).astype(jnp.bfloat16)
    left = np.concatenate([high, high], axis=1)
    table = np.zeros((size_x, RAD), np.float32)
    for i in range(size_x):
        for r in range(RAD):
            place = r - RAD if i < RAD else size_x + r
            if abs(place - i) <= RAD:
                table[i, r] = WEIGHTS[RAD + abs(place - i)]
    slab = pl.BlockSpec((1, size_y, size_z, frames), lambda i: (i, 0, 0, 0))
    side = pl.BlockSpec((RAD, RAD, size_z, frames), lambda i: (i // RAD, 0, 0, 0))
    whole = lambda a, b: pl.BlockSpec((a, b), lambda i: (0, 0))
    half = jax.ShapeDtypeStruct(own.shape, BF16)
    return pl.pallas_call(
        filter_kernel,
        grid=(size_x,),
        in_specs=[
            pl.BlockSpec(memory_space=pltpu.SMEM),
            slab,
            slab,
            pl.BlockSpec((1, size_z, size_y), lambda i: (i, 0, 0)),
            side,
            side,
            whole(size_z, 2 * size_z),
            whole(size_z, size_z),
        ],
        out_specs=[slab, slab, whole(frames // 2 + 8, frames)],
        out_shape=[half, half, jax.ShapeDtypeStruct((frames // 2 + 8, frames), F32)],
        scratch_shapes=[pltpu.VMEM((frames, 2 * frames), F32)],
        compiler_params=pltpu.CompilerParams(vmem_limit_bytes=16 << 20),
        cost_estimate=pl.CostEstimate(
            flops=3_000_000_000, bytes_accessed=13 << 20, transcendentals=0
        ),
        name="filter",
    )(
        jnp.asarray(table),
        part,
        own,
        mask,
        c_before,
        c_after,
        jnp.asarray(left),
        jnp.asarray(low),
    )


def solve_kernel(packed, advance, propagator):
    size = packed.shape[1]
    row = lax.broadcasted_iota(jnp.int32, (size, size), 0)
    lane = lax.broadcasted_iota(jnp.int32, (size, size), 1)
    g = unpack(packed[...], row, lane)
    last = size - 1
    inside = (row < last) & (lane < last)
    diagonal = row == lane
    trace = jnp.sum(jnp.where(diagonal & inside, g, 0.0), axis=(0, 1), keepdims=True)
    lam = trace * (0.5 / last)
    a = jnp.where(inside, g, 0.0) + jnp.where(
        diagonal, jnp.where(row < last, lam, 1.0), 0.0
    )
    wide = jnp.concatenate([a, g], axis=1)
    width = 8
    tiles = [wide[width * t : width * (t + 1)] for t in range(size // width)]
    inner = lax.broadcasted_iota(jnp.int32, (width, 2 * size), 0)

    def doubled(value):
        return jnp.concatenate([value, value], axis=1)

    for t in range(size // width):
        first = t * width
        lines = [tiles[t][i : i + 1] for i in range(width)]
        spread = [
            [
                jnp.broadcast_to(line[:, first + j : first + j + 1], (1, size))
                for j in range(width)
            ]
            for line in lines
        ]
        for i in range(width):
            inverse = 1.0 / spread[i][i]
            lines[i] = lines[i] * doubled(inverse)
            spread[i] = [value * inverse for value in spread[i]]
            for j in range(width):
                if j != i:
                    factor = spread[j][i]
                    lines[j] = lines[j] - doubled(factor) * lines[i]
                    spread[j] = [u - factor * v for u, v in zip(spread[j], spread[i])]
        fresh = []
        for u, tile in enumerate(tiles):
            new = tile
            for i in range(width):
                if u == t:
                    new = jnp.where(inner == i, lines[i], new)
                else:
                    new = new - tile[:, first + i : first + i + 1] * lines[i]
            fresh.append(new)
        tiles = fresh
    b = jnp.concatenate(tiles, axis=0)[:, size:]
    solved = jnp.where(row < last, b, 0.0)
    advance[...] = jnp.where(lane == 0, jnp.where(row == 0, 1.0, 0.0), solved)
    propagator[...] = pltpu.roll(b, last, 1)[:last, :last]


def solve(packed):
    frames = packed.shape[1]
    return pl.pallas_call(
        solve_kernel,
        out_shape=[
            jax.ShapeDtypeStruct((frames, frames), F32),
            jax.ShapeDtypeStruct((frames - 1, frames - 1), F32),
        ],
        compiler_params=pltpu.CompilerParams(vmem_limit_bytes=16 << 20),
        name="solve",
    )(packed)


def fit_kernel(high, low, advance, out):
    m_high, m_low = split(advance[...])
    both = jnp.dot(
        high[...],
        jnp.concatenate([m_high, m_low], axis=1),
        preferred_element_type=F32,
    )
    frames = m_high.shape[0]
    rest = jnp.dot(low[...], m_high, preferred_element_type=F32)
    out[...] = (both[:, :frames] + (both[:, frames:] + rest)).astype(BF16)


def fit(high, low, advance):
    rows, frames = high.shape
    block = 1024
    spec = pl.BlockSpec((block, frames), lambda i: (i, 0))
    return pl.pallas_call(
        fit_kernel,
        grid=(rows // block,),
        in_specs=[spec, spec, pl.BlockSpec((frames, frames), lambda i: (0, 0))],
        out_specs=spec,
        out_shape=jax.ShapeDtypeStruct((rows, frames), BF16),
        compiler_params=pltpu.CompilerParams(vmem_limit_bytes=16 << 20),
        name="fit",
    )(high, low, advance)


def on_device(movie, brain_mask):
    size_x, size_y, size_z, frames = movie.shape
    across = ("y", "x", "c")
    before_high = from_before(movie[size_x - RAD :, size_y - RAD :], "z")
    after_high = from_after(movie[:RAD, size_y - RAD :], "z")
    before_low = from_before(movie[size_x - RAD :, :RAD], "z")
    after_low = from_after(movie[:RAD, :RAD], "z")
    y_before = from_before(movie[:, size_y - RAD :], across)
    y_after = from_after(movie[:, :RAD], across)
    mask = jnp.swapaxes(brain_mask, 1, 2).astype(F32)
    c_before = from_before(jnp.concatenate([before_high, after_high], 0), across)
    c_after = from_after(jnp.concatenate([before_low, after_low], 0), across)
    part = faces(
        movie, y_before, y_after, before_low, before_high, after_low, after_high
    )
    high, low, packed = filter_and_gram(part, movie, mask, c_before, c_after)
    advance, propagator = solve(grid_sum(packed))
    rows = size_x * size_y * size_z
    fitted = fit(high.reshape(rows, frames), low.reshape(rows, frames), advance)
    return fitted.reshape(movie.shape), propagator


def solution(mesh):
    grid = Mesh(mesh.devices.reshape(8, 4, 4, 2), ("z", "y", "x", "c"))
    across = ("y", "x", "c")
    return jax.shard_map(
        on_device,
        mesh=grid,
        in_specs=(P("z", across, None, None), P("z", across, None)),
        out_specs=(P("z", across, None, None), P()),
        check_vma=False,
    )
```

```python
import functools

import jax
import jax.numpy as jnp
import numpy as np
from jax import lax
from jax.experimental import pallas as pl
from jax.experimental.pallas import tpu as pltpu
from jax.sharding import Mesh, PartitionSpec as P

RAD = 4
F32, BF16 = jnp.float32, jnp.bfloat16


def tap_weights():
    offsets = np.arange(-RAD, RAD + 1).astype(np.float64)
    sigma = RAD / 2.0
    raw = np.exp(-offsets * offsets / (2.0 * sigma * sigma))
    return (raw / raw.sum()).astype(np.float32)


WEIGHTS = tap_weights()
TAPS = [float(w) for w in WEIGHTS[RAD:]]


def band_matrix(size):
    band = np.zeros((size, size), np.float32)
    for k in range(-RAD, RAD + 1):
        band += np.diag(np.full(size - abs(k), WEIGHTS[k + RAD]), k)
    return band


def from_before(value, axis):
    size = lax.axis_size(axis)
    return lax.ppermute(value, axis, [(i, i + 1) for i in range(size - 1)])


def from_after(value, axis):
    size = lax.axis_size(axis)
    return lax.ppermute(value, axis, [(i + 1, i) for i in range(size - 1)])


def flipped(value, axis, flip):
    size = lax.axis_size(axis)
    return lax.ppermute(value, axis, [(i, i ^ flip) for i in range(size)])


def pair_sum(value, axis, flip):
    return value + flipped(value, axis, flip)


def quad_sum(value, axis):
    first, second, third = [flipped(value, axis, flip) for flip in (1, 2, 3)]
    return (value + first) + (second + third)


def grid_sum(value):
    value = pair_sum(value, "c", 1)
    for axis in ("x", "y", "z"):
        value = quad_sum(value, axis)
    return pair_sum(value, "z", 6)


def taps_line(line, first, count):
    out = []
    for i in range(first, first + count):
        total = None
        for k, weight in enumerate(TAPS):
            pair = [line[j] for j in sorted({i - k, i + k}) if j in line]
            if not pair:
                continue
            term = (pair[0] if len(pair) == 1 else pair[0] + pair[1]) * weight
            total = term if total is None else total + term
        out.append(total)
    return out


VMEM = pl.BlockSpec(memory_space=pltpu.VMEM)
SMEM = pl.BlockSpec(memory_space=pltpu.SMEM)


def faces_kernel(
    own, y_before, y_after, before_low, before_high, after_low, after_high, out, rows
):
    size_x, size_y, size_z = own.shape[:3]

    @pl.loop(0, size_z // 8)
    def _(step):
        z = pl.ds(pl.multiple_of(step * 8, 8), 8)

        def load(ref, i, j):
            return ref[i, j, z, :].astype(F32)

        def load_line(low, high, i):
            return {
                j: load(low, i, j) if j < RAD else load(high, i, j - RAD)
                for j in range(size_y)
            }

        for i in range(-RAD, size_x + RAD):
            if 0 <= i < size_x:
                line = {j: load(own, i, j) for j in range(size_y)}
                line |= {j - RAD: load(y_before, i, j) for j in range(RAD)}
                line |= {j + size_y: load(y_after, i, j) for j in range(RAD)}
            elif i < 0:
                line = load_line(before_low, before_high, i + RAD)
            else:
                line = load_line(after_low, after_high, i - size_x)
            for j, value in enumerate(taps_line(line, 0, size_y)):
                rows[i + RAD, j] = value
        for j in range(size_y):
            line = {i: rows[i + RAD, j] for i in range(-RAD, size_x + RAD)}
            for i, value in enumerate(taps_line(line, 0, size_x)):
                out[i, j, z, :] = value


def faces(own, y_before, y_after, before_low, before_high, after_low, after_high):
    size_x, size_y, size_z, frames = own.shape
    return pl.pallas_call(
        faces_kernel,
        in_specs=[VMEM] * 7,
        out_specs=VMEM,
        out_shape=jax.ShapeDtypeStruct(own.shape, F32),
        scratch_shapes=[pltpu.VMEM((size_x + 2 * RAD, size_y, 8, frames), F32)],
        compiler_params=pltpu.CompilerParams(vmem_limit_bytes=FACES_VMEM),
        cost_estimate=pl.CostEstimate(
            flops=60_000_000, bytes_accessed=10 << 20, transcendentals=0
        ),
        name="faces",
    )(own, y_before, y_after, before_low, before_high, after_low, after_high)


FACES_VMEM = 16 << 20
FILTER_VMEM = 24 << 20


def split(value):
    high = value.astype(BF16)
    return high, (value - high.astype(F32)).astype(BF16)


def pack(full):
    size = full.shape[0]
    half = size // 2
    row = lax.broadcasted_iota(jnp.int32, (half, size), 0)
    lane = lax.broadcasted_iota(jnp.int32, (half, size), 1)
    moved = pltpu.roll(full[half:], half, 1)
    diagonal = jnp.sum(jnp.where(row == lane, moved, 0.0), axis=0, keepdims=True)
    return jnp.concatenate(
        [
            jnp.where(lane >= row, full[:half], moved),
            jnp.broadcast_to(diagonal, (8, size)),
        ],
        axis=0,
    )


def unpack(packed, row, lane):
    size = packed.shape[1]
    half = size // 2
    top = packed[:half]
    moved = pltpu.roll(top, half, 1)
    inner_row = lax.broadcasted_iota(jnp.int32, (half, size), 0)
    inner_lane = lax.broadcasted_iota(jnp.int32, (half, size), 1)
    diagonal = pltpu.roll(jnp.broadcast_to(packed[half : half + 1], (half, size)), half, 1)
    bottom = jnp.where(inner_lane == inner_row + half, diagonal, moved)
    known = jnp.concatenate([top, bottom], axis=0)
    held = ((row < half) & (lane >= row)) | (
        (row >= half) & (lane >= half) & (lane <= row)
    )
    return jnp.where(held, known, known.T)


def filter_kernel(
    table, part, own, mask, c_before, c_after, left, high_out, low_out, gram, total
):
    size_x, size_y, size_z, frames = own.shape
    total[...] = jnp.zeros_like(total)

    @pl.loop(0, size_x)
    def _(x):
        side = lax.div(x, RAD) * RAD
        weights = [table[x, r] for r in range(RAD)]

        def combined(ref, first, j):
            value = ref[first, j].astype(F32) * weights[0]
            for r in range(1, RAD):
                value = value + ref[first + r, j].astype(F32) * weights[r]
            return value

        lines = {j - RAD: combined(c_before, side, j) for j in range(RAD)}
        lines |= {j + size_y: combined(c_after, side, j) for j in range(RAD)}
        inside = mask[x].astype(F32).T

        def column(j):
            value = part[x, j]
            for i, line in lines.items():
                if abs(i - j) <= RAD:
                    value = value + line * TAPS[abs(i - j)]
            return value

        highs, rests = [], []
        for j in range(0, size_y, 2):
            pair = jnp.concatenate([column(j), column(j + 1)], axis=1)
            high, rest = split(pair)
            blur = jnp.dot(
                left[...],
                jnp.concatenate([high, rest], axis=0),
                preferred_element_type=F32,
            )
            blur = blur[:size_z] + blur[size_z:]
            for q in range(2):
                value = own[x, j + q].astype(F32) - blur[:, q * frames : (q + 1) * frames]
                value = value * inside[:, j + q : j + q + 1]
                high, rest = split(value)
                high_out[x, j + q] = high
                low_out[x, j + q] = rest
                highs.append(high)
                rests.append(rest)
        high = jnp.concatenate(highs, axis=0)
        rest = jnp.concatenate(rests, axis=0)
        total[...] += lax.dot_general(
            high,
            jnp.concatenate([high, rest], axis=1),
            (((0,), (0,)), ((), ())),
            preferred_element_type=F32,
        )

    cross = total[:, frames:]
    gram[...] = pack(total[:, :frames] + (cross + cross.T))


def filter_and_gram(part, own, mask, c_before, c_after):
    size_x, size_y, size_z, frames = own.shape
    band = band_matrix(size_z)
    high = band.astype(jnp.bfloat16)
    low = (band - high.astype(np.float32)).astype(jnp.bfloat16)
    left = np.block([[high, high], [low, low]])
    table = np.zeros((size_x, RAD), np.float32)
    for i in range(size_x):
        for r in range(RAD):
            place = r - RAD if i < RAD else size_x + r
            if abs(place - i) <= RAD:
                table[i, r] = WEIGHTS[RAD + abs(place - i)]
    half = jax.ShapeDtypeStruct(own.shape, BF16)
    return pl.pallas_call(
        filter_kernel,
        in_specs=[SMEM] + [VMEM] * 6,
        out_specs=[VMEM] * 3,
        out_shape=[half, half, jax.ShapeDtypeStruct((frames // 2 + 8, frames), F32)],
        scratch_shapes=[pltpu.VMEM((frames, 2 * frames), F32)],
        compiler_params=pltpu.CompilerParams(vmem_limit_bytes=FILTER_VMEM),
        cost_estimate=pl.CostEstimate(
            flops=3_000_000_000, bytes_accessed=13 << 20, transcendentals=0
        ),
        name="filter",
    )(
        jnp.asarray(table), part, own, mask, c_before, c_after, jnp.asarray(left)
    )


def solve_kernel(packed, advance, propagator):
    size = packed.shape[1]
    row = lax.broadcasted_iota(jnp.int32, (size, size), 0)
    lane = lax.broadcasted_iota(jnp.int32, (size, size), 1)
    g = unpack(packed[...], row, lane)
    last = size - 1
    inside = (row < last) & (lane < last)
    diagonal = row == lane
    trace = jnp.sum(jnp.where(diagonal & inside, g, 0.0), axis=(0, 1), keepdims=True)
    lam = trace * (0.5 / last)
    a = jnp.where(inside, g, 0.0) + jnp.where(
        diagonal, jnp.where(row < last, lam, 1.0), 0.0
    )
    wide = jnp.concatenate([a, g], axis=1)
    width = 8
    tiles = [wide[width * t : width * (t + 1)] for t in range(size // width)]
    inner = lax.broadcasted_iota(jnp.int32, (width, 2 * size), 0)

    def doubled(value):
        return jnp.concatenate([value, value], axis=1)

    for t in range(size // width):
        first = t * width
        lines = [tiles[t][i : i + 1] for i in range(width)]
        spread = [
            [
                jnp.broadcast_to(line[:, first + j : first + j + 1], (1, size))
                for j in range(width)
            ]
            for line in lines
        ]
        for i in range(width):
            inverse = 1.0 / spread[i][i]
            lines[i] = lines[i] * doubled(inverse)
            spread[i] = [value * inverse for value in spread[i]]
            for j in range(width):
                if j != i:
                    factor = spread[j][i]
                    lines[j] = lines[j] - doubled(factor) * lines[i]
                    spread[j] = [u - factor * v for u, v in zip(spread[j], spread[i])]
        fresh = []
        for u, tile in enumerate(tiles):
            new = tile
            for i in range(width):
                if u == t:
                    new = jnp.where(inner == i, lines[i], new)
                else:
                    new = new - tile[:, first + i : first + i + 1] * lines[i]
            fresh.append(new)
        tiles = fresh
    b = jnp.concatenate(tiles, axis=0)[:, size:]
    solved = jnp.where(row < last, b, 0.0)
    advance[...] = jnp.where(lane == 0, jnp.where(row == 0, 1.0, 0.0), solved)
    propagator[...] = pltpu.roll(b, last, 1)[:last, :last]


def solve(packed):
    frames = packed.shape[1]
    return pl.pallas_call(
        solve_kernel,
        out_shape=[
            jax.ShapeDtypeStruct((frames, frames), F32),
            jax.ShapeDtypeStruct((frames - 1, frames - 1), F32),
        ],
        compiler_params=pltpu.CompilerParams(vmem_limit_bytes=16 << 20),
        name="solve",
    )(packed)


def fit_kernel(high, low, advance, out):
    m_high, m_low = split(advance[...])
    frames = m_high.shape[0]
    right = jnp.concatenate(
        [
            jnp.concatenate([m_high, m_low], axis=1),
            jnp.concatenate([m_high, m_low], axis=1),
        ],
        axis=0,
    )
    both = jnp.dot(
        jnp.concatenate([high[...], low[...]], axis=1),
        right,
        preferred_element_type=F32,
    )
    out[...] = (both[:, :frames] + both[:, frames:]).astype(BF16)


def fit(high, low, advance):
    rows, frames = high.shape
    block = 2048
    spec = pl.BlockSpec((block, frames), lambda i: (i, 0))
    return pl.pallas_call(
        fit_kernel,
        grid=(rows // block,),
        in_specs=[spec, spec, pl.BlockSpec((frames, frames), lambda i: (0, 0))],
        out_specs=spec,
        out_shape=jax.ShapeDtypeStruct((rows, frames), BF16),
        compiler_params=pltpu.CompilerParams(vmem_limit_bytes=16 << 20),
        name="fit",
    )(high, low, advance)


def on_device(movie, brain_mask):
    size_x, size_y, size_z, frames = movie.shape
    across = ("y", "x", "c")
    before_high = from_before(movie[size_x - RAD :, size_y - RAD :], "z")
    after_high = from_after(movie[:RAD, size_y - RAD :], "z")
    before_low = from_before(movie[size_x - RAD :, :RAD], "z")
    after_low = from_after(movie[:RAD, :RAD], "z")
    y_before = from_before(movie[:, size_y - RAD :], across)
    y_after = from_after(movie[:, :RAD], across)
    c_before = from_before(jnp.concatenate([before_high, after_high], 0), across)
    c_after = from_after(jnp.concatenate([before_low, after_low], 0), across)
    part = faces(
        movie, y_before, y_after, before_low, before_high, after_low, after_high
    )
    high, low, packed = filter_and_gram(part, movie, brain_mask, c_before, c_after)
    advance, propagator = solve(grid_sum(packed))
    rows = size_x * size_y * size_z
    fitted = fit(high.reshape(rows, frames), low.reshape(rows, frames), advance)
    return fitted.reshape(movie.shape), propagator


def solution(mesh):
    grid = Mesh(mesh.devices.reshape(8, 4, 4, 2), ("z", "y", "x", "c"))
    across = ("y", "x", "c")
    return jax.shard_map(
        on_device,
        mesh=grid,
        in_specs=(P("z", across, None, None), P("z", across, None)),
        out_specs=(P("z", across, None, None), P()),
        check_vma=False,
    )
```

```python
import functools

import jax
import jax.numpy as jnp
import numpy as np
from jax import lax
from jax.experimental import pallas as pl
from jax.experimental.pallas import tpu as pltpu
from jax.sharding import Mesh, PartitionSpec as P

RAD = 4
F32, BF16 = jnp.float32, jnp.bfloat16


def tap_weights():
    offsets = np.arange(-RAD, RAD + 1).astype(np.float64)
    sigma = RAD / 2.0
    raw = np.exp(-offsets * offsets / (2.0 * sigma * sigma))
    return (raw / raw.sum()).astype(np.float32)


WEIGHTS = tap_weights()
TAPS = [float(w) for w in WEIGHTS[RAD:]]


def band_matrix(size):
    band = np.zeros((size, size), np.float32)
    for k in range(-RAD, RAD + 1):
        band += np.diag(np.full(size - abs(k), WEIGHTS[k + RAD]), k)
    return band


def from_before(value, axis):
    size = lax.axis_size(axis)
    return lax.ppermute(value, axis, [(i, i + 1) for i in range(size - 1)])


def from_after(value, axis):
    size = lax.axis_size(axis)
    return lax.ppermute(value, axis, [(i + 1, i) for i in range(size - 1)])


def flipped(value, axis, flip):
    size = lax.axis_size(axis)
    return lax.ppermute(value, axis, [(i, i ^ flip) for i in range(size)])


def pair_sum(value, axis, flip):
    return value + flipped(value, axis, flip)


def quad_sum(value, axis):
    first, second, third = [flipped(value, axis, flip) for flip in (1, 2, 3)]
    return (value + first) + (second + third)


def grid_sum(value):
    value = pair_sum(value, "c", 1)
    for axis in ("x", "y", "z"):
        value = quad_sum(value, axis)
    return pair_sum(value, "z", 6)


def taps_line(line, first, count):
    out = []
    for i in range(first, first + count):
        total = None
        for k, weight in enumerate(TAPS):
            pair = [line[j] for j in sorted({i - k, i + k}) if j in line]
            if not pair:
                continue
            term = (pair[0] if len(pair) == 1 else pair[0] + pair[1]) * weight
            total = term if total is None else total + term
        out.append(total)
    return out


VMEM = pl.BlockSpec(memory_space=pltpu.VMEM)
SMEM = pl.BlockSpec(memory_space=pltpu.SMEM)


def faces_kernel(
    own, y_after, y_before, before_low, before_high, after_low, after_high, out, rows
):
    size_x, size_y, size_z = own.shape[:3]

    @pl.loop(0, size_z // 8)
    def _(step):
        z = pl.ds(pl.multiple_of(step * 8, 8), 8)

        def load(ref, i, j):
            return ref[i, j, z, :].astype(F32)

        def load_line(low, high, i):
            return {
                j: load(low, i, j) if j < RAD else load(high, i, j - RAD)
                for j in range(size_y)
            }

        for i in range(-RAD, size_x + RAD):
            if 0 <= i < size_x:
                line = {j: load(own, i, j) for j in range(size_y)}
                line |= {j - RAD: load(y_before, i, j) for j in range(RAD)}
                line |= {j + size_y: load(y_after, i, j) for j in range(RAD)}
            elif i < 0:
                line = load_line(before_low, before_high, i + RAD)
            else:
                line = load_line(after_low, after_high, i - size_x)
            for j, value in enumerate(taps_line(line, 0, size_y)):
                rows[i + RAD, j] = value
        for j in range(size_y):
            line = {i: rows[i + RAD, j] for i in range(-RAD, size_x + RAD)}
            for i, value in enumerate(taps_line(line, 0, size_x)):
                out[i, j, z, :] = value


def faces(own, y_before, y_after, before_low, before_high, after_low, after_high):
    size_x, size_y, size_z, frames = own.shape
    return pl.pallas_call(
        faces_kernel,
        in_specs=[VMEM] * 7,
        out_specs=VMEM,
        out_shape=jax.ShapeDtypeStruct(own.shape, F32),
        scratch_shapes=[pltpu.VMEM((size_x + 2 * RAD, size_y, 8, frames), F32)],
        compiler_params=pltpu.CompilerParams(vmem_limit_bytes=FACES_VMEM),
        cost_estimate=pl.CostEstimate(
            flops=60_000_000, bytes_accessed=10 << 20, transcendentals=0
        ),
        name="faces",
    )(own, y_after, y_before, before_low, before_high, after_low, after_high)


FACES_VMEM = 16 << 20
FILTER_VMEM = 24 << 20


def split(value):
    high = value.astype(BF16)
    return high, (value - high.astype(F32)).astype(BF16)


def pack(full):
    size = full.shape[0]
    half = size // 2
    row = lax.broadcasted_iota(jnp.int32, (half, size), 0)
    lane = lax.broadcasted_iota(jnp.int32, (half, size), 1)
    moved = pltpu.roll(full[half:], half, 1)
    diagonal = jnp.sum(jnp.where(row == lane, moved, 0.0), axis=0, keepdims=True)
    return jnp.concatenate(
        [
            jnp.where(lane >= row, full[:half], moved),
            jnp.broadcast_to(diagonal, (8, size)),
        ],
        axis=0,
    )


def unpack(packed, row, lane):
    size = packed.shape[1]
    half = size // 2
    top = packed[:half]
    moved = pltpu.roll(top, half, 1)
    inner_row = lax.broadcasted_iota(jnp.int32, (half, size), 0)
    inner_lane = lax.broadcasted_iota(jnp.int32, (half, size), 1)
    diagonal = pltpu.roll(jnp.broadcast_to(packed[half : half + 1], (half, size)), half, 1)
    bottom = jnp.where(inner_lane == inner_row + half, diagonal, moved)
    known = jnp.concatenate([top, bottom], axis=0)
    held = ((row < half) & (lane >= row)) | (
        (row >= half) & (lane >= half) & (lane <= row)
    )
    return jnp.where(held, known, known.T)


def filter_kernel(
    table, part, own, mask, c_before, c_after, left, high_out, low_out, gram, total
):
    size_x, size_y, size_z, frames = own.shape
    total[...] = jnp.zeros_like(total)

    @pl.loop(0, size_x, unroll=4)
    def _(x):
        side = lax.div(x, RAD) * RAD
        weights = [table[x, r] for r in range(RAD)]

        def combined(ref, first, j):
            value = ref[first, j].astype(F32) * weights[0]
            for r in range(1, RAD):
                value = value + ref[first + r, j].astype(F32) * weights[r]
            return value

        lines = {j - RAD: combined(c_before, side, j) for j in range(RAD)}
        lines |= {j + size_y: combined(c_after, side, j) for j in range(RAD)}
        inside = mask[x].astype(F32).T

        def column(j):
            value = part[x, j]
            for i, line in lines.items():
                if abs(i - j) <= RAD:
                    value = value + line * TAPS[abs(i - j)]
            return value

        highs, rests = [], []
        for j in range(0, size_y, 2):
            pair = jnp.concatenate([column(j), column(j + 1)], axis=1)
            high, rest = split(pair)
            blur = jnp.dot(
                left[...],
                jnp.concatenate([high, rest], axis=0),
                preferred_element_type=F32,
            )
            blur = blur[:size_z] + blur[size_z:]
            for q in range(2):
                value = own[x, j + q].astype(F32) - blur[:, q * frames : (q + 1) * frames]
                value = value * inside[:, j + q : j + q + 1]
                high, rest = split(value)
                high_out[x, j + q] = high
                low_out[x, j + q] = rest
                highs.append(high)
                rests.append(rest)
        high = jnp.concatenate(highs, axis=0)
        rest = jnp.concatenate(rests, axis=0)
        total[...] += lax.dot_general(
            high,
            jnp.concatenate([high, rest], axis=1),
            (((0,), (0,)), ((), ())),
            preferred_element_type=F32,
        )

    cross = total[:, frames:]
    gram[...] = pack(total[:, :frames] + (cross + cross.T))


def filter_and_gram(part, own, mask, c_before, c_after):
    size_x, size_y, size_z, frames = own.shape
    band = band_matrix(size_z)
    high = band.astype(jnp.bfloat16)
    low = (band - high.astype(np.float32)).astype(jnp.bfloat16)
    left = np.block([[high, high], [low, low]])
    table = np.zeros((size_x, RAD), np.float32)
    for i in range(size_x):
        for r in range(RAD):
            place = r - RAD if i < RAD else size_x + r
            if abs(place - i) <= RAD:
                table[i, r] = WEIGHTS[RAD + abs(place - i)]
    half = jax.ShapeDtypeStruct(own.shape, BF16)
    return pl.pallas_call(
        filter_kernel,
        in_specs=[SMEM] + [VMEM] * 6,
        out_specs=[VMEM] * 3,
        out_shape=[half, half, jax.ShapeDtypeStruct((frames // 2 + 8, frames), F32)],
        scratch_shapes=[pltpu.VMEM((frames, 2 * frames), F32)],
        compiler_params=pltpu.CompilerParams(vmem_limit_bytes=FILTER_VMEM),
        cost_estimate=pl.CostEstimate(
            flops=3_000_000_000, bytes_accessed=13 << 20, transcendentals=0
        ),
        name="filter",
    )(
        jnp.asarray(table), part, own, mask, c_before, c_after, jnp.asarray(left)
    )


def solve_kernel(packed, advance, propagator):
    size = packed.shape[1]
    row = lax.broadcasted_iota(jnp.int32, (size, size), 0)
    lane = lax.broadcasted_iota(jnp.int32, (size, size), 1)
    g = unpack(packed[...], row, lane)
    last = size - 1
    inside = (row < last) & (lane < last)
    diagonal = row == lane
    trace = jnp.sum(jnp.where(diagonal & inside, g, 0.0), axis=(0, 1), keepdims=True)
    lam = trace * (0.5 / last)
    a = jnp.where(inside, g, 0.0) + jnp.where(
        diagonal, jnp.where(row < last, lam, 1.0), 0.0
    )
    wide = jnp.concatenate([a, g], axis=1)
    width = 8
    tiles = [wide[width * t : width * (t + 1)] for t in range(size // width)]
    inner = lax.broadcasted_iota(jnp.int32, (width, 2 * size), 0)

    def doubled(value):
        return jnp.concatenate([value, value], axis=1)

    for t in range(size // width):
        first = t * width
        lines = [tiles[t][i : i + 1] for i in range(width)]
        spread = [
            [
                jnp.broadcast_to(line[:, first + j : first + j + 1], (1, size))
                for j in range(width)
            ]
            for line in lines
        ]
        for i in range(width):
            inverse = 1.0 / spread[i][i]
            lines[i] = lines[i] * doubled(inverse)
            spread[i] = [value * inverse for value in spread[i]]
            for j in range(width):
                if j != i:
                    factor = spread[j][i]
                    lines[j] = lines[j] - doubled(factor) * lines[i]
                    spread[j] = [u - factor * v for u, v in zip(spread[j], spread[i])]
        fresh = []
        for u, tile in enumerate(tiles):
            new = tile
            for i in range(width):
                if u == t:
                    new = jnp.where(inner == i, lines[i], new)
                else:
                    new = new - tile[:, first + i : first + i + 1] * lines[i]
            fresh.append(new)
        tiles = fresh
    b = jnp.concatenate(tiles, axis=0)[:, size:]
    solved = jnp.where(row < last, b, 0.0)
    advance[...] = jnp.where(lane == 0, jnp.where(row == 0, 1.0, 0.0), solved)
    propagator[...] = pltpu.roll(b, last, 1)[:last, :last]


def solve(packed):
    frames = packed.shape[1]
    return pl.pallas_call(
        solve_kernel,
        out_shape=[
            jax.ShapeDtypeStruct((frames, frames), F32),
            jax.ShapeDtypeStruct((frames - 1, frames - 1), F32),
        ],
        compiler_params=pltpu.CompilerParams(vmem_limit_bytes=16 << 20),
        name="solve",
    )(packed)


FIT_PIECES = 8


def fit_kernel(high, low, advance, out, held, sems):
    rows = high.shape[0] // FIT_PIECES
    m_high, m_low = split(advance[...])
    frames = m_high.shape[0]
    right = jnp.concatenate([m_high, m_low], axis=1)
    right = jnp.concatenate([right, right], axis=0)
    copies = []
    for i in range(FIT_PIECES):
        piece = pl.ds(i * rows, rows)
        both = jnp.dot(
            jnp.concatenate([high[piece, :], low[piece, :]], axis=1),
            right,
            preferred_element_type=F32,
        )
        held[i] = (both[:, :frames] + both[:, frames:]).astype(BF16)
        copy = pltpu.make_async_copy(held.at[i], out.at[piece, :], sems.at[i])
        copy.start()
        copies.append(copy)
    for copy in copies:
        copy.wait()


def fit(high, low, advance):
    rows, frames = high.shape
    return pl.pallas_call(
        fit_kernel,
        in_specs=[VMEM] * 3,
        out_specs=pl.BlockSpec(memory_space=pl.ANY),
        out_shape=jax.ShapeDtypeStruct((rows, frames), BF16),
        scratch_shapes=[
            pltpu.VMEM((FIT_PIECES, rows // FIT_PIECES, frames), BF16),
            pltpu.SemaphoreType.DMA((FIT_PIECES,)),
        ],
        compiler_params=pltpu.CompilerParams(vmem_limit_bytes=16 << 20),
        name="fit",
    )(high, low, advance)


def on_device(movie, brain_mask):
    size_x, size_y, size_z, frames = movie.shape
    across = ("y", "x", "c")
    before_high = from_before(movie[size_x - RAD :, size_y - RAD :], "z")
    after_high = from_after(movie[:RAD, size_y - RAD :], "z")
    before_low = from_before(movie[size_x - RAD :, :RAD], "z")
    after_low = from_after(movie[:RAD, :RAD], "z")
    y_before = from_before(movie[:, size_y - RAD :], across)
    y_after = from_after(movie[:, :RAD], across)
    c_before = from_before(jnp.concatenate([before_high, after_high], 0), across)
    c_after = from_after(jnp.concatenate([before_low, after_low], 0), across)
    part = faces(
        movie, y_before, y_after, before_low, before_high, after_low, after_high
    )
    high, low, packed = filter_and_gram(part, movie, brain_mask, c_before, c_after)
    advance, propagator = solve(grid_sum(packed))
    rows = size_x * size_y * size_z
    fitted = fit(high.reshape(rows, frames), low.reshape(rows, frames), advance)
    return fitted.reshape(movie.shape), propagator


def solution(mesh):
    grid = Mesh(mesh.devices.reshape(8, 4, 4, 2), ("z", "y", "x", "c"))
    across = ("y", "x", "c")
    return jax.shard_map(
        on_device,
        mesh=grid,
        in_specs=(P("z", across, None, None), P("z", across, None)),
        out_specs=(P("z", across, None, None), P()),
        check_vma=False,
    )
```

```python
import functools

import jax
import jax.numpy as jnp
import numpy as np
from jax import lax
from jax.experimental import pallas as pl
from jax.experimental.pallas import tpu as pltpu
from jax.sharding import Mesh, PartitionSpec as P

RAD = 4
F32, BF16 = jnp.float32, jnp.bfloat16


def tap_weights():
    offsets = np.arange(-RAD, RAD + 1).astype(np.float64)
    sigma = RAD / 2.0
    raw = np.exp(-offsets * offsets / (2.0 * sigma * sigma))
    return (raw / raw.sum()).astype(np.float32)


WEIGHTS = tap_weights()
TAPS = [float(w) for w in WEIGHTS[RAD:]]


def band_matrix(size):
    band = np.zeros((size, size), np.float32)
    for k in range(-RAD, RAD + 1):
        band += np.diag(np.full(size - abs(k), WEIGHTS[k + RAD]), k)
    return band


def from_before(value, axis):
    size = lax.axis_size(axis)
    return lax.ppermute(value, axis, [(i, (i + 1) % size) for i in range(size)])


def from_after(value, axis):
    size = lax.axis_size(axis)
    return lax.ppermute(value, axis, [((i + 1) % size, i) for i in range(size)])


def inner_sides(x_axis, y_axis):
    side = jnp.arange(4)
    place = jnp.where(side < 2, lax.axis_index(x_axis), lax.axis_index(y_axis))
    ends = np.array([0, lax.axis_size(x_axis) - 1, 0, lax.axis_size(y_axis) - 1])
    return (place != ends).astype(F32)


def flipped(value, axis, flip):
    size = lax.axis_size(axis)
    return lax.ppermute(value, axis, [(i, i ^ flip) for i in range(size)])


def pair_sum(value, axis, flip):
    return value + flipped(value, axis, flip)


def quad_sum(value, axis):
    first, second, third = [flipped(value, axis, flip) for flip in (1, 2, 3)]
    return (value + first) + (second + third)


def grid_sum(value):
    value = pair_sum(value, "c", 1)
    for axis in ("x", "y", "z"):
        value = quad_sum(value, axis)
    return pair_sum(value, "z", 6)


def taps_line(line, first, count):
    out = []
    for i in range(first, first + count):
        total = None
        for k, weight in enumerate(TAPS):
            pair = [line[j] for j in sorted({i - k, i + k}) if j in line]
            if not pair:
                continue
            term = (pair[0] if len(pair) == 1 else pair[0] + pair[1]) * weight
            total = term if total is None else total + term
        out.append(total)
    return out


VMEM = pl.BlockSpec(memory_space=pltpu.VMEM)
SMEM = pl.BlockSpec(memory_space=pltpu.SMEM)


def faces_kernel(
    sides, own, y_before, y_after, before_low, before_high, after_low, after_high, out, rows
):
    size_x, size_y, size_z = own.shape[:3]

    @pl.loop(0, size_z // 8)
    def _(step):
        z = pl.ds(pl.multiple_of(step * 8, 8), 8)

        def load(ref, i, j):
            return ref[i, j, z, :].astype(F32)

        def load_line(low, high, i):
            return {
                j: load(low, i, j) if j < RAD else load(high, i, j - RAD)
                for j in range(size_y)
            }

        for i in range(-RAD, size_x + RAD):
            if 0 <= i < size_x:
                line = {j: load(own, i, j) for j in range(size_y)}
                line |= {j - RAD: load(y_before, i, j) * sides[2] for j in range(RAD)}
                line |= {j + size_y: load(y_after, i, j) * sides[3] for j in range(RAD)}
            elif i < 0:
                line = load_line(before_low, before_high, i + RAD)
            else:
                line = load_line(after_low, after_high, i - size_x)
            for j, value in enumerate(taps_line(line, 0, size_y)):
                if i < 0:
                    value = value * sides[0]
                elif i >= size_x:
                    value = value * sides[1]
                rows[i + RAD, j] = value
        for j in range(size_y):
            line = {i: rows[i + RAD, j] for i in range(-RAD, size_x + RAD)}
            for i, value in enumerate(taps_line(line, 0, size_x)):
                out[i, j, z, :] = value


def faces(sides, own, y_before, y_after, before_low, before_high, after_low, after_high):
    size_x, size_y, size_z, frames = own.shape
    return pl.pallas_call(
        faces_kernel,
        in_specs=[SMEM] + [VMEM] * 7,
        out_specs=VMEM,
        out_shape=jax.ShapeDtypeStruct(own.shape, F32),
        scratch_shapes=[pltpu.VMEM((size_x + 2 * RAD, size_y, 8, frames), F32)],
        compiler_params=pltpu.CompilerParams(vmem_limit_bytes=FACES_VMEM),
        cost_estimate=pl.CostEstimate(
            flops=60_000_000, bytes_accessed=10 << 20, transcendentals=0
        ),
        name="faces",
    )(sides, own, y_before, y_after, before_low, before_high, after_low, after_high)


FACES_VMEM = 16 << 20
FILTER_VMEM = 24 << 20


def split(value):
    high = value.astype(BF16)
    return high, (value - high.astype(F32)).astype(BF16)


def pack(full):
    size = full.shape[0]
    half = size // 2
    row = lax.broadcasted_iota(jnp.int32, (half, size), 0)
    lane = lax.broadcasted_iota(jnp.int32, (half, size), 1)
    moved = pltpu.roll(full[half:], half, 1)
    diagonal = jnp.sum(jnp.where(row == lane, moved, 0.0), axis=0, keepdims=True)
    return jnp.concatenate(
        [
            jnp.where(lane >= row, full[:half], moved),
            jnp.broadcast_to(diagonal, (8, size)),
        ],
        axis=0,
    )


def unpack(packed, row, lane):
    size = packed.shape[1]
    half = size // 2
    top = packed[:half]
    moved = pltpu.roll(top, half, 1)
    inner_row = lax.broadcasted_iota(jnp.int32, (half, size), 0)
    inner_lane = lax.broadcasted_iota(jnp.int32, (half, size), 1)
    diagonal = pltpu.roll(jnp.broadcast_to(packed[half : half + 1], (half, size)), half, 1)
    bottom = jnp.where(inner_lane == inner_row + half, diagonal, moved)
    known = jnp.concatenate([top, bottom], axis=0)
    held = ((row < half) & (lane >= row)) | (
        (row >= half) & (lane >= half) & (lane <= row)
    )
    return jnp.where(held, known, known.T)


def filter_kernel(
    sides, table, part, own, mask, left, *refs
):
    first_before, first_after, last_before, last_after, *refs = refs
    high_out, low_out, gram, total = refs
    size_x, size_y, size_z, frames = own.shape
    total[...] = jnp.zeros_like(total)

    def slab(x, side, c_before, c_after):
        def combined(ref, weights, j):
            value = ref[0, j].astype(F32) * weights[0]
            for r in range(1, RAD):
                value = value + ref[r, j].astype(F32) * weights[r]
            return value

        before, after = [
            [table[x, r] * (sides[side] * sides[q]) for r in range(RAD)] for q in (2, 3)
        ]
        lines = {j - RAD: combined(c_before, before, j) for j in range(RAD)}
        lines |= {j + size_y: combined(c_after, after, j) for j in range(RAD)}
        inside = mask[x].astype(F32).T

        def column(j):
            value = part[x, j]
            for i, line in lines.items():
                if abs(i - j) <= RAD:
                    value = value + line * TAPS[abs(i - j)]
            return value

        highs, rests = [], []
        for j in range(0, size_y, 2):
            pair = jnp.concatenate([column(j), column(j + 1)], axis=1)
            high, rest = split(pair)
            blur = jnp.dot(
                left[...],
                jnp.concatenate([high, rest], axis=0),
                preferred_element_type=F32,
            )
            blur = blur[:size_z] + blur[size_z:]
            for q in range(2):
                value = own[x, j + q].astype(F32) - blur[:, q * frames : (q + 1) * frames]
                value = value * inside[:, j + q : j + q + 1]
                high, rest = split(value)
                high_out[x, j + q] = high
                low_out[x, j + q] = rest
                highs.append(high)
                rests.append(rest)
        high = jnp.concatenate(highs, axis=0)
        rest = jnp.concatenate(rests, axis=0)
        total[...] += lax.dot_general(
            high,
            jnp.concatenate([high, rest], axis=1),
            (((0,), (0,)), ((), ())),
            preferred_element_type=F32,
        )

    @pl.loop(0, RAD, unroll=True)
    def _(x):
        slab(x, 0, first_before, first_after)

    @pl.loop(RAD, size_x, unroll=True)
    def _(x):
        slab(x, 1, last_before, last_after)

    cross = total[:, frames:]
    gram[...] = pack(total[:, :frames] + (cross + cross.T))


def filter_and_gram(sides, part, own, mask, corners):
    size_x, size_y, size_z, frames = own.shape
    band = band_matrix(size_z)
    high = band.astype(jnp.bfloat16)
    low = (band - high.astype(np.float32)).astype(jnp.bfloat16)
    left = np.block([[high, high], [low, low]])
    table = np.zeros((size_x, RAD), np.float32)
    for i in range(size_x):
        for r in range(RAD):
            place = r - RAD if i < RAD else size_x + r
            if abs(place - i) <= RAD:
                table[i, r] = WEIGHTS[RAD + abs(place - i)]
    half = jax.ShapeDtypeStruct(own.shape, BF16)
    return pl.pallas_call(
        filter_kernel,
        in_specs=[SMEM] * 2 + [VMEM] * 8,
        out_specs=[VMEM] * 3,
        out_shape=[half, half, jax.ShapeDtypeStruct((frames // 2 + 8, frames), F32)],
        scratch_shapes=[pltpu.VMEM((frames, 2 * frames), F32)],
        compiler_params=pltpu.CompilerParams(vmem_limit_bytes=FILTER_VMEM),
        cost_estimate=pl.CostEstimate(
            flops=3_000_000_000, bytes_accessed=13 << 20, transcendentals=0
        ),
        name="filter",
    )(
        sides, jnp.asarray(table), part, own, mask, jnp.asarray(left), *corners
    )


def solve_kernel(packed, advance, propagator):
    size = packed.shape[1]
    row = lax.broadcasted_iota(jnp.int32, (size, size), 0)
    lane = lax.broadcasted_iota(jnp.int32, (size, size), 1)
    g = unpack(packed[...], row, lane)
    last = size - 1
    inside = (row < last) & (lane < last)
    diagonal = row == lane
    trace = jnp.sum(jnp.where(diagonal & inside, g, 0.0), axis=(0, 1), keepdims=True)
    lam = trace * (0.5 / last)
    a = jnp.where(inside, g, 0.0) + jnp.where(
        diagonal, jnp.where(row < last, lam, 1.0), 0.0
    )
    wide = jnp.concatenate([a, g], axis=1)
    width = 8
    tiles = [wide[width * t : width * (t + 1)] for t in range(size // width)]
    inner = lax.broadcasted_iota(jnp.int32, (width, 2 * size), 0)

    def doubled(value):
        return jnp.concatenate([value, value], axis=1)

    for t in range(size // width):
        first = t * width
        lines = [tiles[t][i : i + 1] for i in range(width)]
        spread = [
            [
                jnp.broadcast_to(line[:, first + j : first + j + 1], (1, size))
                for j in range(width)
            ]
            for line in lines
        ]
        for i in range(width):
            inverse = 1.0 / spread[i][i]
            lines[i] = lines[i] * doubled(inverse)
            spread[i] = [value * inverse for value in spread[i]]
            for j in range(width):
                if j != i:
                    factor = spread[j][i]
                    lines[j] = lines[j] - doubled(factor) * lines[i]
                    spread[j] = [u - factor * v for u, v in zip(spread[j], spread[i])]
        fresh = []
        for u, tile in enumerate(tiles):
            new = tile
            for i in range(width):
                if u == t:
                    new = jnp.where(inner == i, lines[i], new)
                else:
                    new = new - tile[:, first + i : first + i + 1] * lines[i]
            fresh.append(new)
        tiles = fresh
    b = jnp.concatenate(tiles, axis=0)[:, size:]
    solved = jnp.where(row < last, b, 0.0)
    advance[...] = jnp.where(lane == 0, jnp.where(row == 0, 1.0, 0.0), solved)
    propagator[...] = pltpu.roll(b, last, 1)[:last, :last]


def solve(packed):
    frames = packed.shape[1]
    return pl.pallas_call(
        solve_kernel,
        out_shape=[
            jax.ShapeDtypeStruct((frames, frames), F32),
            jax.ShapeDtypeStruct((frames - 1, frames - 1), F32),
        ],
        compiler_params=pltpu.CompilerParams(vmem_limit_bytes=16 << 20),
        name="solve",
    )(packed)


FIT_PIECES = 8


def fit_kernel(high, low, advance, out, held, sems):
    rows = high.shape[0] // FIT_PIECES
    m_high, m_low = split(advance[...])
    frames = m_high.shape[0]
    right = jnp.concatenate([m_high, m_low], axis=1)
    right = jnp.concatenate([right, right], axis=0)
    copies = []
    for i in range(FIT_PIECES):
        piece = pl.ds(i * rows, rows)
        both = jnp.dot(
            jnp.concatenate([high[piece, :], low[piece, :]], axis=1),
            right,
            preferred_element_type=F32,
        )
        held[i] = (both[:, :frames] + both[:, frames:]).astype(BF16)
        copy = pltpu.make_async_copy(held.at[i], out.at[piece, :], sems.at[i])
        copy.start()
        copies.append(copy)
    for copy in copies:
        copy.wait()


def fit(high, low, advance):
    rows, frames = high.shape
    return pl.pallas_call(
        fit_kernel,
        in_specs=[VMEM] * 3,
        out_specs=pl.BlockSpec(memory_space=pl.ANY),
        out_shape=jax.ShapeDtypeStruct((rows, frames), BF16),
        scratch_shapes=[
            pltpu.VMEM((FIT_PIECES, rows // FIT_PIECES, frames), BF16),
            pltpu.SemaphoreType.DMA((FIT_PIECES,)),
        ],
        compiler_params=pltpu.CompilerParams(vmem_limit_bytes=16 << 20),
        name="fit",
    )(high, low, advance)


def on_device(movie, brain_mask):
    size_x, size_y, size_z, frames = movie.shape
    across = ("y", "x", "c")
    def held(*values):
        return lax.optimization_barrier((movie, *values))[0]

    source = movie
    last_high, first_low = source[size_x - RAD :, size_y - RAD :], source[:RAD, :RAD]
    before_high = from_before(last_high, "z")
    after_low = from_after(first_low, "z")
    source = held(last_high, first_low)
    y_last, y_first = source[:, size_y - RAD :], source[:, :RAD]
    y_before = from_before(y_last, across)
    y_after = from_after(y_first, across)
    source = held(y_last, y_first)
    before_low = from_before(source[size_x - RAD :, :RAD], "z")
    after_high = from_after(source[:RAD, size_y - RAD :], "z")
    corners = (
        from_before(before_high, across),
        from_after(before_low, across),
        from_before(after_high, across),
        from_after(after_low, across),
    )
    sides = inner_sides("z", across)
    part = faces(
        sides, movie, y_before, y_after, before_low, before_high, after_low, after_high
    )
    high, low, packed = filter_and_gram(sides, part, movie, brain_mask, corners)
    advance, propagator = solve(grid_sum(packed))
    rows = size_x * size_y * size_z
    fitted = fit(high.reshape(rows, frames), low.reshape(rows, frames), advance)
    return fitted.reshape(movie.shape), propagator


def solution(mesh):
    grid = Mesh(mesh.devices.reshape(8, 4, 4, 2), ("z", "y", "x", "c"))
    across = ("y", "x", "c")
    return jax.shard_map(
        on_device,
        mesh=grid,
        in_specs=(P("z", across, None, None), P("z", across, None)),
        out_specs=(P("z", across, None, None), P()),
        check_vma=False,
    )
```

```python
import functools

import jax
import jax.numpy as jnp
import numpy as np
from jax import lax
from jax.experimental import pallas as pl
from jax.experimental.pallas import tpu as pltpu
from jax.sharding import Mesh, PartitionSpec as P

RAD = 4
F32, BF16 = jnp.float32, jnp.bfloat16


def tap_weights():
    offsets = np.arange(-RAD, RAD + 1).astype(np.float64)
    sigma = RAD / 2.0
    raw = np.exp(-offsets * offsets / (2.0 * sigma * sigma))
    return (raw / raw.sum()).astype(np.float32)


WEIGHTS = tap_weights()
TAPS = [float(w) for w in WEIGHTS[RAD:]]


def band_matrix(size):
    band = np.zeros((size, size), np.float32)
    for k in range(-RAD, RAD + 1):
        band += np.diag(np.full(size - abs(k), WEIGHTS[k + RAD]), k)
    return band


def from_before(value, axis):
    size = lax.axis_size(axis)
    return lax.ppermute(value, axis, [(i, (i + 1) % size) for i in range(size)])


def from_after(value, axis):
    size = lax.axis_size(axis)
    return lax.ppermute(value, axis, [((i + 1) % size, i) for i in range(size)])


def inner_sides():
    sides = []
    for axes in (("z",), ("y", "x", "c")):
        first, last = True, True
        for axis in axes:
            index = lax.axis_index(axis)
            first = first & (index == 0)
            last = last & (index == lax.axis_size(axis) - 1)
        sides += [jnp.where(first, 0.0, 1.0), jnp.where(last, 0.0, 1.0)]
    return sides


def flipped(value, axis, flip):
    size = lax.axis_size(axis)
    return lax.ppermute(value, axis, [(i, i ^ flip) for i in range(size)])


def pair_sum(value, axis, flip):
    return value + flipped(value, axis, flip)


def quad_sum(value, axis):
    first, second, third = [flipped(value, axis, flip) for flip in (1, 2, 3)]
    return (value + first) + (second + third)


def grid_sum(value):
    value = pair_sum(value, "c", 1)
    for axis in ("x", "y", "z"):
        value = quad_sum(value, axis)
    return pair_sum(value, "z", 6)


def taps_line(line, first, count):
    out = []
    for i in range(first, first + count):
        total = None
        for k, weight in enumerate(TAPS):
            pair = [line[j] for j in sorted({i - k, i + k}) if j in line]
            if not pair:
                continue
            term = (pair[0] if len(pair) == 1 else pair[0] + pair[1]) * weight
            total = term if total is None else total + term
        out.append(total)
    return out


VMEM = pl.BlockSpec(memory_space=pltpu.VMEM)
SMEM = pl.BlockSpec(memory_space=pltpu.SMEM)


def faces_kernel(
    own, y_before, y_after, before_low, before_high, after_low, after_high, out, rows
):
    size_x, size_y, size_z = own.shape[:3]
    frames = own.shape[3]
    inner = [jnp.full((8, frames), side, F32) for side in inner_sides()]

    @pl.loop(0, size_z // 8)
    def _(step):
        z = pl.ds(pl.multiple_of(step * 8, 8), 8)

        def load(ref, i, j):
            return ref[i, j, z, :].astype(F32)

        def load_line(low, high, i):
            return {
                j: load(low, i, j) if j < RAD else load(high, i, j - RAD)
                for j in range(size_y)
            }

        for i in range(-RAD, size_x + RAD):
            if 0 <= i < size_x:
                line = {j: load(own, i, j) for j in range(size_y)}
                line |= {j - RAD: load(y_before, i, j) * inner[2] for j in range(RAD)}
                line |= {j + size_y: load(y_after, i, j) * inner[3] for j in range(RAD)}
            elif i < 0:
                line = load_line(before_low, before_high, i + RAD)
            else:
                line = load_line(after_low, after_high, i - size_x)
            for j, value in enumerate(taps_line(line, 0, size_y)):
                if i < 0:
                    value = value * inner[0]
                elif i >= size_x:
                    value = value * inner[1]
                rows[i + RAD, j] = value
        for j in range(size_y):
            line = {i: rows[i + RAD, j] for i in range(-RAD, size_x + RAD)}
            for i, value in enumerate(taps_line(line, 0, size_x)):
                out[i, j, z, :] = value


def faces(own, y_before, y_after, before_low, before_high, after_low, after_high):
    size_x, size_y, size_z, frames = own.shape
    return pl.pallas_call(
        faces_kernel,
        in_specs=[VMEM] * 7,
        out_specs=VMEM,
        out_shape=jax.ShapeDtypeStruct(own.shape, F32),
        scratch_shapes=[pltpu.VMEM((size_x + 2 * RAD, size_y, 8, frames), F32)],
        compiler_params=pltpu.CompilerParams(vmem_limit_bytes=FACES_VMEM),
        cost_estimate=pl.CostEstimate(
            flops=60_000_000, bytes_accessed=10 << 20, transcendentals=0
        ),
        name="faces",
    )(own, y_before, y_after, before_low, before_high, after_low, after_high)


FACES_VMEM = 16 << 20
FILTER_VMEM = 24 << 20


def split(value):
    high = value.astype(BF16)
    return high, (value - high.astype(F32)).astype(BF16)


def pack(full):
    size = full.shape[0]
    half = size // 2
    row = lax.broadcasted_iota(jnp.int32, (half, size), 0)
    lane = lax.broadcasted_iota(jnp.int32, (half, size), 1)
    moved = pltpu.roll(full[half:], half, 1)
    diagonal = jnp.sum(jnp.where(row == lane, moved, 0.0), axis=0, keepdims=True)
    return jnp.concatenate(
        [
            jnp.where(lane >= row, full[:half], moved),
            jnp.broadcast_to(diagonal, (8, size)),
        ],
        axis=0,
    )


def unpack(packed, row, lane):
    size = packed.shape[1]
    half = size // 2
    top = packed[:half]
    moved = pltpu.roll(top, half, 1)
    inner_row = lax.broadcasted_iota(jnp.int32, (half, size), 0)
    inner_lane = lax.broadcasted_iota(jnp.int32, (half, size), 1)
    diagonal = pltpu.roll(jnp.broadcast_to(packed[half : half + 1], (half, size)), half, 1)
    bottom = jnp.where(inner_lane == inner_row + half, diagonal, moved)
    known = jnp.concatenate([top, bottom], axis=0)
    held = ((row < half) & (lane >= row)) | (
        (row >= half) & (lane >= half) & (lane <= row)
    )
    return jnp.where(held, known, known.T)


def filter_kernel(
    table, part, own, mask, left, *refs
):
    first_before, first_after, last_before, last_after, *refs = refs
    high_out, low_out, gram, total = refs
    size_x, size_y, size_z, frames = own.shape
    total[...] = jnp.zeros_like(total)
    sides = inner_sides()

    def slab(x, side, c_before, c_after):
        def combined(ref, weights, j):
            value = ref[0, j].astype(F32) * weights[0]
            for r in range(1, RAD):
                value = value + ref[r, j].astype(F32) * weights[r]
            return value

        before, after = [
            [table[x, r] * (sides[side] * sides[q]) for r in range(RAD)] for q in (2, 3)
        ]
        lines = {j - RAD: combined(c_before, before, j) for j in range(RAD)}
        lines |= {j + size_y: combined(c_after, after, j) for j in range(RAD)}
        inside = mask[x].astype(F32).T

        def column(j):
            value = part[x, j]
            for i, line in lines.items():
                if abs(i - j) <= RAD:
                    value = value + line * TAPS[abs(i - j)]
            return value

        highs, rests = [], []
        for j in range(0, size_y, 2):
            pair = jnp.concatenate([column(j), column(j + 1)], axis=1)
            high, rest = split(pair)
            blur = jnp.dot(
                left[...],
                jnp.concatenate([high, rest], axis=0),
                preferred_element_type=F32,
            )
            blur = blur[:size_z] + blur[size_z:]
            for q in range(2):
                value = own[x, j + q].astype(F32) - blur[:, q * frames : (q + 1) * frames]
                value = value * inside[:, j + q : j + q + 1]
                high, rest = split(value)
                high_out[x, j + q] = high
                low_out[x, j + q] = rest
                highs.append(high)
                rests.append(rest)
        high = jnp.concatenate(highs, axis=0)
        rest = jnp.concatenate(rests, axis=0)
        total[...] += lax.dot_general(
            high,
            jnp.concatenate([high, rest], axis=1),
            (((0,), (0,)), ((), ())),
            preferred_element_type=F32,
        )

    @pl.loop(0, RAD, unroll=True)
    def _(x):
        slab(x, 0, first_before, first_after)

    @pl.loop(RAD, size_x, unroll=True)
    def _(x):
        slab(x, 1, last_before, last_after)

    cross = total[:, frames:]
    gram[...] = pack(total[:, :frames] + (cross + cross.T))


def filter_and_gram(part, own, mask, corners):
    size_x, size_y, size_z, frames = own.shape
    band = band_matrix(size_z)
    high = band.astype(jnp.bfloat16)
    low = (band - high.astype(np.float32)).astype(jnp.bfloat16)
    left = np.block([[high, high], [low, low]])
    table = np.zeros((size_x, RAD), np.float32)
    for i in range(size_x):
        for r in range(RAD):
            place = r - RAD if i < RAD else size_x + r
            if abs(place - i) <= RAD:
                table[i, r] = WEIGHTS[RAD + abs(place - i)]
    half = jax.ShapeDtypeStruct(own.shape, BF16)
    return pl.pallas_call(
        filter_kernel,
        in_specs=[SMEM] + [VMEM] * 8,
        out_specs=[VMEM] * 3,
        out_shape=[half, half, jax.ShapeDtypeStruct((frames // 2 + 8, frames), F32)],
        scratch_shapes=[pltpu.VMEM((frames, 2 * frames), F32)],
        compiler_params=pltpu.CompilerParams(vmem_limit_bytes=FILTER_VMEM),
        cost_estimate=pl.CostEstimate(
            flops=3_000_000_000, bytes_accessed=13 << 20, transcendentals=0
        ),
        name="filter",
    )(
        jnp.asarray(table), part, own, mask, jnp.asarray(left), *corners
    )


def solve_kernel(packed, advance, propagator):
    size = packed.shape[1]
    row = lax.broadcasted_iota(jnp.int32, (size, size), 0)
    lane = lax.broadcasted_iota(jnp.int32, (size, size), 1)
    g = unpack(packed[...], row, lane)
    last = size - 1
    inside = (row < last) & (lane < last)
    diagonal = row == lane
    trace = jnp.sum(jnp.where(diagonal & inside, g, 0.0), axis=(0, 1), keepdims=True)
    lam = trace * (0.5 / last)
    a = jnp.where(inside, g, 0.0) + jnp.where(
        diagonal, jnp.where(row < last, lam, 1.0), 0.0
    )
    wide = jnp.concatenate([a, g], axis=1)
    width = 8
    tiles = [wide[width * t : width * (t + 1)] for t in range(size // width)]
    inner = lax.broadcasted_iota(jnp.int32, (width, 2 * size), 0)

    def doubled(value):
        return jnp.concatenate([value, value], axis=1)

    for t in range(size // width):
        first = t * width
        lines = [tiles[t][i : i + 1] for i in range(width)]
        spread = [
            [
                jnp.broadcast_to(line[:, first + j : first + j + 1], (1, size))
                for j in range(width)
            ]
            for line in lines
        ]
        for i in range(width):
            inverse = 1.0 / spread[i][i]
            lines[i] = lines[i] * doubled(inverse)
            spread[i] = [value * inverse for value in spread[i]]
            for j in range(width):
                if j != i:
                    factor = spread[j][i]
                    lines[j] = lines[j] - doubled(factor) * lines[i]
                    spread[j] = [u - factor * v for u, v in zip(spread[j], spread[i])]
        fresh = []
        for u, tile in enumerate(tiles):
            new = tile
            for i in range(width):
                if u == t:
                    new = jnp.where(inner == i, lines[i], new)
                else:
                    new = new - tile[:, first + i : first + i + 1] * lines[i]
            fresh.append(new)
        tiles = fresh
    b = jnp.concatenate(tiles, axis=0)[:, size:]
    solved = jnp.where(row < last, b, 0.0)
    advance[...] = jnp.where(lane == 0, jnp.where(row == 0, 1.0, 0.0), solved)
    propagator[...] = pltpu.roll(b, last, 1)[:last, :last]


def solve(packed):
    frames = packed.shape[1]
    return pl.pallas_call(
        solve_kernel,
        out_shape=[
            jax.ShapeDtypeStruct((frames, frames), F32),
            jax.ShapeDtypeStruct((frames - 1, frames - 1), F32),
        ],
        compiler_params=pltpu.CompilerParams(vmem_limit_bytes=16 << 20),
        name="solve",
    )(packed)


FIT_PIECES = 8


def fit_kernel(high, low, advance, out, held, sems):
    rows = high.shape[0] // FIT_PIECES
    m_high, m_low = split(advance[...])
    frames = m_high.shape[0]
    right = jnp.concatenate([m_high, m_low], axis=1)
    right = jnp.concatenate([right, right], axis=0)
    copies = []
    for i in range(FIT_PIECES):
        piece = pl.ds(i * rows, rows)
        both = jnp.dot(
            jnp.concatenate([high[piece, :], low[piece, :]], axis=1),
            right,
            preferred_element_type=F32,
        )
        held[i] = (both[:, :frames] + both[:, frames:]).astype(BF16)
        copy = pltpu.make_async_copy(held.at[i], out.at[piece, :], sems.at[i])
        copy.start()
        copies.append(copy)
    for copy in copies:
        copy.wait()


def fit(high, low, advance):
    rows, frames = high.shape
    return pl.pallas_call(
        fit_kernel,
        in_specs=[VMEM] * 3,
        out_specs=pl.BlockSpec(memory_space=pl.ANY),
        out_shape=jax.ShapeDtypeStruct((rows, frames), BF16),
        scratch_shapes=[
            pltpu.VMEM((FIT_PIECES, rows // FIT_PIECES, frames), BF16),
            pltpu.SemaphoreType.DMA((FIT_PIECES,)),
        ],
        compiler_params=pltpu.CompilerParams(vmem_limit_bytes=16 << 20),
        name="fit",
    )(high, low, advance)


def on_device(movie, brain_mask):
    size_x, size_y, size_z, frames = movie.shape
    across = ("y", "x", "c")
    def held(*values):
        return lax.optimization_barrier((movie, *values))[0]

    source = movie
    last_high, first_low = source[size_x - RAD :, size_y - RAD :], source[:RAD, :RAD]
    before_high = from_before(last_high, "z")
    after_low = from_after(first_low, "z")
    source = held(last_high, first_low)
    y_last, y_first = source[:, size_y - RAD :], source[:, :RAD]
    y_before = from_before(y_last, across)
    y_after = from_after(y_first, across)
    source = held(y_last, y_first)
    before_low = from_before(source[size_x - RAD :, :RAD], "z")
    after_high = from_after(source[:RAD, size_y - RAD :], "z")
    corners = (
        from_before(before_high, across),
        from_after(before_low, across),
        from_before(after_high, across),
        from_after(after_low, across),
    )
    part = faces(
        movie, y_before, y_after, before_low, before_high, after_low, after_high
    )
    high, low, packed = filter_and_gram(part, movie, brain_mask, corners)
    advance, propagator = solve(grid_sum(packed))
    rows = size_x * size_y * size_z
    fitted = fit(high.reshape(rows, frames), low.reshape(rows, frames), advance)
    return fitted.reshape(movie.shape), propagator


def solution(mesh):
    grid = Mesh(mesh.devices.reshape(8, 4, 4, 2), ("z", "y", "x", "c"))
    across = ("y", "x", "c")
    return jax.shard_map(
        on_device,
        mesh=grid,
        in_specs=(P("z", across, None, None), P("z", across, None)),
        out_specs=(P("z", across, None, None), P()),
        check_vma=False,
    )
```
